128 devices in a mesh: region: 128 (over x, y, z, core).
Axes of the slice: x: 4, y: 4, z: 4, core: 2. Of those that a mesh axis runs over, the one named last changes fastest.
Arguments:
- node_feat: bfloat16 [65536, 512], P('region'), may hold values from -6 to 6
- edge_feat: bfloat16 [524288, 512], P('region'), may hold values from -6 to 6
- sender: int32 [524288], P('region'), may hold values from 0 to 2815, as said below
- receiver: int32 [524288], P('region'), may hold values from 0 to 512, as said below
- send_list: int32 [128, 8, 32], P('region'), may hold values from 16 to 511
- edge_w1: bfloat16 [1536, 512], replicated, may hold values from -0.15625 to 0.15625
- edge_b1: float32 [512], replicated, may hold values from -4 to 4
- edge_w2: bfloat16 [512, 512], replicated, may hold values from -0.25 to 0.25
- edge_b2: float32 [512], replicated, may hold values from -4 to 4
- edge_gain: float32 [512], replicated, may hold values from 0.5 to 1.5
- edge_shift: float32 [512], replicated, may hold values from -4 to 4
- node_w1: bfloat16 [1024, 512], replicated, may hold values from -0.1875 to 0.1875
- node_b1: float32 [512], replicated, may hold values from -4 to 4
- node_w2: bfloat16 [512, 512], replicated, may hold values from -0.25 to 0.25
- node_b2: float32 [512], replicated, may hold values from -4 to 4
- node_gain: float32 [512], replicated, may hold values from 0.5 to 1.5
- node_shift: float32 [512], replicated, may hold values from -4 to 4
Outputs:
- edge_out: bfloat16 [524288, 512], P('region')
- node_out: bfloat16 [65536, 512], P('region')
The draws below stay inside these ranges and needn't reach their ends.
Inputs may be any that keep to these rules, and one draw needn't show every extreme that they name: `sender`: a row of the region's table as built in the first step; every region has slots pointing at row 0 and at the last row. `receiver`: non-decreasing within each region's 4096 slots; the value 512 marks an empty slot, and empty slots stand after the used ones; some region uses all its slots. `send_list`: entry [s, j, k] is a local index on region s of a node that s sends to its j-th neighbour.
All inputs are finite; a program needn't handle non-finite values.
Results may differ from the reference program's by a relative error of at most 0.0043.
Values may be sent and summed in bfloat16 or wider, within the bound.
No kernel may reach another device: no remote copies, remote signals or barrier semaphores. Data moves between devices by JAX's collectives and lax.ppermute only.
A program may use at most 128 MiB of HBM per device.

```python
import jax
import jax.numpy as jnp
from jax import lax

D = 512
NODE_DEV = 512
EDGE_DEV = 4096
COARSE_DEV = 16
NEIGH = 8
SLOT = 32
NODES = 65536
EDGES = 524288
TABLE = 2816
N_REGION = 128


def draw_sender(key, part):
    keys = jax.random.split(jax.random.fold_in(key, 11), 5)
    shape = (N_REGION, EDGE_DEV)
    kinds = jax.random.randint(keys[0], shape, 0, 10)
    local = jax.random.randint(keys[1], shape, 0, NODE_DEV)
    coarse = NODE_DEV + jax.random.randint(keys[2], shape, 0, COARSE_DEV * N_REGION)
    halo = NODE_DEV + COARSE_DEV * N_REGION + jax.random.randint(keys[3], shape, 0, NEIGH * SLOT)
    picked = jnp.where(kinds < 6, local, jnp.where(kinds < 8, coarse, halo))
    forced = jax.random.randint(keys[4], (N_REGION, 1), 0, EDGE_DEV)
    column = jnp.arange(EDGE_DEV, dtype=jnp.int32)[None, :]
    picked = jnp.where(column == forced, TABLE - 1, picked)
    picked = jnp.where(column == (forced + 1) % EDGE_DEV, 0, picked)
    return picked.reshape(-1).astype(jnp.int32)


def draw_receiver(key, part):
    keys = jax.random.split(jax.random.fold_in(key, 23), 3)
    levels = jax.random.randint(keys[0], (N_REGION,), 0, 4)
    divisor = jnp.array([1, 2, 4, 8], dtype=jnp.int32)[levels]
    live = EDGE_DEV // divisor
    full = jax.random.randint(keys[1], (), 0, N_REGION)
    rows = jnp.arange(N_REGION, dtype=jnp.int32)
    live = jnp.where(rows == full, EDGE_DEV, jnp.where(rows == (full + 1) % N_REGION, EDGE_DEV // 2, live))
    base = jnp.sort(jax.random.randint(keys[2], (N_REGION, EDGE_DEV), 0, NODE_DEV), axis=1)
    column = jnp.arange(EDGE_DEV, dtype=jnp.int32)[None, :]
    where_from = jnp.minimum(column * EDGE_DEV // live[:, None], EDGE_DEV - 1)
    chosen = jnp.take_along_axis(base, where_from, axis=1)
    chosen = jnp.where(column == 0, 0, chosen)
    chosen = jnp.where(column < live[:, None], chosen, NODE_DEV)
    return chosen.reshape(-1).astype(jnp.int32)


def set_ends(values, rng, smallest, top_value):
    place = [jax.random.randint(jax.random.fold_in(rng, axis), (), 0, length) for axis, length in enumerate(values.shape)]
    main_axis = values.shape.index(max(values.shape))
    neighbour = place[:main_axis] + [(place[main_axis] + 1) % values.shape[main_axis]] + place[main_axis + 1:]
    return values.at[tuple(place)].set(smallest).at[tuple(neighbour)].set(top_value)


def steps_of(stream_key, shape, cuts, low, top_value):
    def one(axis_at, blocks):
        draws = jax.random.uniform(jax.random.fold_in(jax.random.fold_in(stream_key, 6), axis_at), (blocks,), jnp.float32, low / len(cuts), top_value / len(cuts))
        return jnp.repeat(jnp.exp(draws), shape[axis_at] // blocks).reshape((-1,) + (1,) * (len(shape) - axis_at - 1))

    factor_of = one(*cuts[0])
    for cut in cuts[1:]:
        factor_of = factor_of * one(*cut)
    return factor_of


def noise(key, extent, width, most, cuts=(), kind=jnp.bfloat16):
    drawn = jax.random.normal(key, extent, jnp.float32) * width
    if len(cuts) > 0:
        drawn = steps_of(key, extent, cuts, -0.22, 0.18) * drawn
    return jnp.clip(drawn, min=-most, max=most).astype(kind)


def setup_inputs(seed: int = 0) -> dict:
    key_of = jax.random.split(jax.random.key(seed), 18)
    node_feat = noise(key_of[0], (NODES, D), 1.0, 6.0, ((0, 128),))
    edge_feat = noise(key_of[1], (EDGES, D), 1.0, 6.0, ((0, 128),))
    sender = draw_sender(jax.random.fold_in(key_of[17], 71), 0)
    receiver = draw_receiver(jax.random.fold_in(key_of[17], 71), 0)
    send_list = set_ends(jax.random.randint(key_of[4], (N_REGION, NEIGH, SLOT), COARSE_DEV, NODE_DEV), jax.random.fold_in(key_of[4], 1), COARSE_DEV, NODE_DEV - 1).astype(jnp.int32)
    edge_w1 = noise(key_of[5], (3 * D, D), (3 * D) ** -0.5, 0.15625)
    edge_b1 = noise(key_of[6], (D,), 1.0, 4.0, (), jnp.float32)
    edge_w2 = noise(key_of[7], (D, D), D ** -0.5, 0.25)
    edge_b2 = noise(key_of[8], (D,), 1.0, 4.0, (), jnp.float32)
    edge_gain = jnp.clip(1.0 + 0.1 * jax.random.normal(key_of[9], (D,), jnp.float32), 0.5, 1.5)
    edge_shift = noise(key_of[10], (D,), 1.0, 4.0, (), jnp.float32)
    node_w1 = noise(key_of[11], (2 * D, D), (2 * D) ** -0.5, 0.1875)
    node_b1 = noise(key_of[12], (D,), 1.0, 4.0, (), jnp.float32)
    node_w2 = noise(key_of[13], (D, D), D ** -0.5, 0.25)
    node_b2 = noise(key_of[14], (D,), 1.0, 4.0, (), jnp.float32)
    node_gain = jnp.clip(1.0 + 0.1 * jax.random.normal(key_of[15], (D,), jnp.float32), 0.5, 1.5)
    node_shift = noise(key_of[16], (D,), 1.0, 4.0, (), jnp.float32)
    return dict(node_feat=node_feat, edge_feat=edge_feat, sender=sender, receiver=receiver, send_list=send_list, edge_w1=edge_w1, edge_b1=edge_b1, edge_w2=edge_w2, edge_b2=edge_b2, edge_gain=edge_gain, edge_shift=edge_shift, node_w1=node_w1, node_b1=node_b1, node_w2=node_w2, node_b2=node_b2, node_gain=node_gain, node_shift=node_shift)


NEIGHBOUR_STEPS = (1, -1, 7, -7, 8, -8, 9, -9)

def network(inputs, w_first, b_first, w_second, b_second, gain, shift):
    pre = jnp.dot(inputs, w_first, preferred_element_type=jnp.float32) + b_first
    hidden = jax.nn.silu(pre).astype(jnp.bfloat16)
    out = jnp.dot(hidden, w_second, preferred_element_type=jnp.float32) + b_second
    mean = lax.optimization_barrier(jnp.mean(out, axis=-1, keepdims=True))
    var = lax.optimization_barrier(jnp.mean((out - mean) ** 2, axis=-1, keepdims=True))
    return (out - mean) * lax.rsqrt(var + 1e-05) * gain + shift

def reference(node_feat, edge_feat, sender, receiver, send_list, edge_w1, edge_b1, edge_w2, edge_b2, edge_gain, edge_shift, node_w1, node_b1, node_w2, node_b2, node_gain, node_shift):
    node_all = node_feat.reshape(N_REGION, NODE_DEV, D)
    edge_all = edge_feat.reshape(N_REGION, EDGE_DEV, D)
    send_all = sender.reshape(N_REGION, EDGE_DEV)
    recv_all = receiver.reshape(N_REGION, EDGE_DEV)
    coarse_all = node_all[:, :COARSE_DEV].reshape(-1, D)
    distances = jnp.array(NEIGHBOUR_STEPS, dtype=jnp.int32)
    positions = jnp.arange(NEIGH, dtype=jnp.int32)

    def region_update(region):
        local = node_all[region]
        sources = (region - distances) % N_REGION
        picks = send_list[sources, positions]
        halo = node_all[sources[:, None], picks].reshape(-1, D)
        table = jnp.concatenate([local, coarse_all, halo], axis=0)
        edges = edge_all[region]
        senders = send_all[region]
        receivers = recv_all[region]
        live = receivers < NODE_DEV
        recv_rows = jnp.take(local, jnp.minimum(receivers, NODE_DEV - 1), axis=0)
        inputs = jnp.concatenate([edges, jnp.take(table, senders, axis=0), recv_rows], axis=1)
        update = network(inputs, edge_w1, edge_b1, edge_w2, edge_b2, edge_gain, edge_shift)
        new_edges = jnp.where(live[:, None], edges.astype(jnp.float32) + update, 0.0).astype(jnp.bfloat16)
        aggregate = jax.ops.segment_sum(new_edges.astype(jnp.float32), receivers, num_segments=NODE_DEV + 1)[:NODE_DEV]
        node_in = jnp.concatenate([local, aggregate.astype(jnp.bfloat16)], axis=1)
        node_update = network(node_in, node_w1, node_b1, node_w2, node_b2, node_gain, node_shift)
        new_nodes = (local.astype(jnp.float32) + node_update).astype(jnp.bfloat16)
        return (new_edges, new_nodes)
    new_edges, new_nodes = lax.map(region_update, jnp.arange(N_REGION, dtype=jnp.int32))
    return (new_edges.reshape(EDGES, D), new_nodes.reshape(NODES, D))
```

```python
import functools

import jax
import jax.numpy as jnp
from jax import lax
from jax.experimental import pallas as pl
from jax.experimental.pallas import tpu as pltpu
from jax.sharding import PartitionSpec as P

COARSE_DEV = 16
BLOCK = 512
WINDOW = 128
PHASES = ((2, 1, 0), (0, 2, 1))


def coords_of(region):
    return [region >> 5 & 3, region >> 3 & 3, region >> 1 & 3, region & 1]


def region_of(x, y, z, core):
    return ((x * 4 + y) * 4 + z) * 2 + core


def ring_route(phase, step):
    route = []
    for region in range(128):
        place = coords_of(region)
        dim = PHASES[place[3]][phase]
        place[dim] = (place[dim] + step) % 4
        route.append((region, region_of(*place)))
    return route


def linear_route(step):
    return [(i, (i + step) % 128) for i in range(128)]


def gather_coarse(coarse):
    held = coarse
    for phase in range(3):
        parts = [held]
        parts += [lax.ppermute(held, "region", ring_route(phase, k)) for k in (1, 2, 3)]
        held = jnp.concatenate(parts, axis=0)
    other = lax.ppermute(held, "region", [(i, i ^ 1) for i in range(128)])
    return held, other


def coarse_places(index):
    me = lax.axis_index("region")
    mine = coords_of(me)
    row = index & 15
    theirs = coords_of(index >> 4)
    rel = [(mine[d] - theirs[d]) & 3 for d in range(3)]
    order = [(rel[c] * 16 + rel[b] * 4 + rel[a]) for a, b, c in PHASES]
    block = jnp.where(theirs[3] == 0, order[0], order[1])
    return jnp.where(theirs[3] == mine[3], 0, 1024) + block * 16 + row


def exchange_halo(rows):
    up = lax.ppermute(
        jnp.concatenate([rows[4], rows[6], rows[2]], 0), "region", linear_route(8)
    )
    down = lax.ppermute(
        jnp.concatenate([rows[5], rows[3], rows[7]], 0), "region", linear_route(-8)
    )
    right = lax.ppermute(
        jnp.concatenate([rows[0], up[32:64], down[32:64]], 0), "region", linear_route(1)
    )
    left = lax.ppermute(
        jnp.concatenate([rows[1], up[64:96], down[64:96]], 0), "region", linear_route(-1)
    )
    return up, down, right, left


def layer_norm_update(hidden, w_ref, b_ref, gain_ref, shift_ref):
    y = jnp.dot(hidden, w_ref[...], preferred_element_type=jnp.float32) + b_ref[...]
    mean = jnp.mean(y, axis=-1, keepdims=True)
    d = y - mean
    var = jnp.mean(d * d, axis=-1, keepdims=True)
    return d * lax.rsqrt(var + 1e-05) * gain_ref[...] + shift_ref[...]


def half_silu(u):
    return (u + u * jnp.tanh(u)).astype(jnp.bfloat16)


def layer_kernel(
    send_ref, recv_ref, live_ref,
    recv_row, edge, node, own, other, up, down, right, left,
    w1, b1, w2, b2, gain, shift, nw1, nb1, nw2, nb2, ngain, nshift,
    edge_out, node_out,
    ts, tr, g, acc,
):
    step = pl.program_id(0)

    def project(src, count, w_lo, dst, first, bias):
        for lo in range(0, count, 256):
            n = min(256, count - lo)
            res = jnp.dot(
                src[lo : lo + n, :], w1[w_lo : w_lo + 512, :],
                preferred_element_type=jnp.float32,
            )
            if bias is not None:
                res = res + bias[...]
            for j in range(4):
                dst[pl.ds((first + lo) * 4 + j, n, stride=4), :] = res[:, j * 128 : j * 128 + 128]

    @pl.when(step == 0)
    def _():
        acc[...] = jnp.zeros_like(acc)
        tr[512 * 4 :, :] = jnp.zeros((tr.shape[0] - 2048, 128), jnp.float32)
        project(node, 512, 1024, tr, 0, b1)
        project(node, 512, 512, ts, 0, None)
        project(own, 1024, 512, ts, 512, None)
        project(other, 1024, 512, ts, 1536, None)
        project(up, 96, 512, ts, 2560, None)
        project(down, 96, 512, ts, 2656, None)
        project(right, 96, 512, ts, 2752, None)
        project(left, 96, 512, ts, 2848, None)

    first = step * BLOCK

    def fetch(e, carry):
        s = pl.multiple_of(send_ref[first + e] * 4, 4)
        r = pl.multiple_of(recv_ref[first + e] * 4, 4)
        g[pl.ds(pl.multiple_of(e * 4, 4), 4), :] = ts[pl.ds(s, 4), :] + tr[pl.ds(r, 4), :]
        return carry

    lax.fori_loop(0, BLOCK, fetch, 0, unroll=16)

    feat = edge[...]
    pre = jnp.dot(feat, w1[0:512, :], preferred_element_type=jnp.float32)
    gathered = jnp.concatenate([g[pl.ds(j, BLOCK, stride=4), :] for j in range(4)], axis=1)
    hidden = half_silu(0.5 * (pre + gathered))
    update = layer_norm_update(hidden, w2, b2, gain, shift)
    slot = first + lax.broadcasted_iota(jnp.int32, (BLOCK, 1), 0)
    result = jnp.where(slot < live_ref[0], feat.astype(jnp.float32) + update, 0.0).astype(jnp.bfloat16)
    edge_out[...] = result

    low = recv_ref[first] >> 3 << 3
    high = recv_ref[first + BLOCK - 1]

    def add_window(k, carry):
        base = pl.multiple_of(low + k * WINDOW, 8)
        ids = base + lax.broadcasted_iota(jnp.int32, (WINDOW, BLOCK), 0)
        one_hot = jnp.where(ids == recv_row[0], 1.0, 0.0).astype(jnp.bfloat16)
        acc[pl.ds(base, WINDOW), :] += jnp.dot(one_hot, edge_out[...], preferred_element_type=jnp.float32)
        return carry

    lax.fori_loop(0, (high - low) // WINDOW + 1, add_window, 0)

    @pl.when(step == pl.num_programs(0) - 1)
    def _():
        feat = node[...]
        pre = (
            jnp.dot(feat, nw1[0:512, :], preferred_element_type=jnp.float32)
            + jnp.dot(acc[0:512, :].astype(jnp.bfloat16), nw1[512:1024, :], preferred_element_type=jnp.float32)
            + nb1[...]
        )
        update = layer_norm_update(half_silu(0.5 * pre), nw2, nb2, ngain, nshift)
        node_out[...] = (feat.astype(jnp.float32) + update).astype(jnp.bfloat16)


def on_device(
    node_feat, edge_feat, sender, receiver, send_list,
    edge_w1, edge_b1, edge_w2, edge_b2, edge_gain, edge_shift,
    node_w1, node_b1, node_w2, node_b2, node_gain, node_shift,
):
    ids = jnp.arange(512, dtype=jnp.int32)
    pick = (send_list.reshape(256, 1) == ids[None, :]).astype(jnp.bfloat16)
    rows = jnp.dot(pick, node_feat, preferred_element_type=jnp.float32).astype(jnp.bfloat16)
    rows = rows.reshape(8, 32, 512)
    own, other = gather_coarse(node_feat[:COARSE_DEV])
    up, down, right, left = exchange_halo(rows)

    h = sender - 2560
    slot = h >> 5
    starts = (2752, 2848, 2880, 2816, 2560, 2656, 2784, 2912)
    start = jnp.full_like(sender, starts[0])
    for j in range(1, 8):
        start = jnp.where(slot == j, starts[j], start)
    place = jnp.where(
        sender < 512,
        sender,
        jnp.where(sender < 2560, 512 + coarse_places(sender - 512), start + (h & 31)),
    )
    live = jnp.sum((receiver < 512).astype(jnp.int32)).reshape(1)

    blocks = 4096 // BLOCK
    whole = lambda a: pl.BlockSpec(a.shape, lambda i, *_: (0,) * a.ndim, pipeline_mode=pl.Buffered(1))
    row = lambda a: a.reshape(1, -1)
    fixed = [
        node_feat, own, other, up, down, right, left,
        edge_w1, row(edge_b1), edge_w2, row(edge_b2), row(edge_gain), row(edge_shift),
        node_w1, row(node_b1), node_w2, row(node_b2), row(node_gain), row(node_shift),
    ]
    return pl.pallas_call(
        layer_kernel,
        grid_spec=pltpu.PrefetchScalarGridSpec(
            num_scalar_prefetch=3,
            grid=(blocks,),
            in_specs=[
                pl.BlockSpec((1, 1, BLOCK), lambda i, *_: (i, 0, 0)),
                pl.BlockSpec((BLOCK, 512), lambda i, *_: (i, 0)),
            ]
            + [whole(a) for a in fixed],
            out_specs=[
                pl.BlockSpec((BLOCK, 512), lambda i, *_: (i, 0)),
                pl.BlockSpec((512, 512), lambda i, *_: (0, 0)),
            ],
            scratch_shapes=[
                pltpu.VMEM((2944 * 4, 128), jnp.float32),
                pltpu.VMEM((520 * 4, 128), jnp.float32),
                pltpu.VMEM((BLOCK * 4, 128), jnp.float32),
                pltpu.VMEM((640, 512), jnp.float32),
            ],
        ),
        out_shape=[
            jax.ShapeDtypeStruct((4096, 512), jnp.bfloat16),
            jax.ShapeDtypeStruct((512, 512), jnp.bfloat16),
        ],
    )(place, receiver, live, receiver.reshape(blocks, 1, BLOCK), edge_feat, *fixed)


def solution(mesh):
    sharded = {0: P("region", None), 1: P("region", None), 2: P("region"), 3: P("region"), 4: P("region", None, None)}
    in_specs = tuple(sharded.get(i, P()) for i in range(17))
    out_specs = (P("region", None), P("region", None))
    step = lambda *a: tuple(on_device(*a))
    return jax.shard_map(step, mesh=mesh, in_specs=in_specs, out_specs=out_specs, check_vma=False)
```

```python
import jax
import jax.numpy as jnp
from jax import lax
from jax.experimental import pallas as pl
from jax.experimental.pallas import tpu as pltpu
from jax.sharding import PartitionSpec as P

COARSE_DEV = 16
BLOCK = 512
WINDOW = 128
HALF = BLOCK // 2
CHUNK = 64
OWN, OTHER, UP, DOWN, NEXT, SWAP, ROWS = 512, 1536, 2560, 2656, 2752, 2848, 2944
PHASES = ((2, 1, 0), (0, 2, 1))


def coords_of(region):
    return [region >> 5 & 3, region >> 3 & 3, region >> 1 & 3, region & 1]


def region_of(x, y, z, core):
    return ((x * 4 + y) * 4 + z) * 2 + core


def ring_route(phase, step):
    route = []
    for region in range(128):
        place = coords_of(region)
        dim = PHASES[place[3]][phase]
        place[dim] = (place[dim] + step) % 4
        route.append((region, region_of(*place)))
    return route


def linear_route(step):
    return [(i, (i + step) % 128) for i in range(128)]


def ring_phase(held, phase):
    parts = [held]
    parts += [lax.ppermute(held, "region", ring_route(phase, k)) for k in (1, 2, 3)]
    return jnp.concatenate(parts, axis=0)


def shifted(blocks, step):
    return lax.ppermute(jnp.concatenate(blocks, 0), "region", linear_route(step))


def coarse_places(index):
    me = lax.axis_index("region")
    mine = coords_of(me)
    row = index & 15
    theirs = coords_of(index >> 4)
    rel = [(mine[d] - theirs[d]) & 3 for d in range(3)]
    order = [(rel[c] * 16 + rel[b] * 4 + rel[a]) for a, b, c in PHASES]
    block = jnp.where(theirs[3] == 0, order[0], order[1])
    return jnp.where(theirs[3] == mine[3], 0, 1024) + block * 16 + row


def normed(y, gain_ref, shift_ref):
    mean = jnp.mean(y, axis=-1, keepdims=True)
    d = y - mean
    var = jnp.mean(d * d, axis=-1, keepdims=True)
    return d * lax.rsqrt(var + 1e-05) * gain_ref[...] + shift_ref[...]


def half_silu(u):
    return (u + u * jnp.tanh(u)).astype(jnp.bfloat16)


def dot(a, b):
    return jnp.dot(a, b, preferred_element_type=jnp.float32)


def window_hits(base, recv_row):
    ids = base + lax.broadcasted_iota(jnp.int32, (WINDOW, BLOCK), 0)
    return jnp.where(ids == recv_row, 1.0, 0.0).astype(jnp.bfloat16)


def project(src, lo, count, at, w1, ts):
    for r in range(0, count, 256):
        n = min(256, count - r)
        res = 0.5 * dot(src[lo + r : lo + r + n, :], w1[512:1024, :])
        for j in range(4):
            ts[pl.ds((at + r) * 4 + j, n, stride=4), :] = res[:, j * 128 : j * 128 + 128]


def first_kernel(
    node, w1, nw1, edge, nb1, recv_rows,
    node_v, w1_v, edge_v, high, low_bits, ts, node_part, bounds,
    nw_top, sems,
):
    moves = [(node, node_v), (w1, w1_v), (nw1.at[0:512, :], nw_top), (edge, edge_v)]
    copies = [pltpu.make_async_copy(a, b, sems.at[i]) for i, (a, b) in enumerate(moves)]
    for copy in copies:
        copy.start()
    recv = recv_rows[:, 0, :]
    used = jnp.where(recv < 512, 1, 0)
    bounds[16] = jnp.sum(used)
    for b in range(4096 // BLOCK):
        low = jnp.min(recv[b : b + 1, :]) >> 3 << 3
        bounds[b] = low
        bounds[8 + b] = (jnp.max(recv[b : b + 1, :]) - low) // WINDOW + 1
    copies[0].wait()
    copies[1].wait()
    tr = 0.5 * dot(node_v[...], w1_v[1024:1536, :])
    top = tr.astype(jnp.bfloat16)
    high[0:512, :] = top
    low_bits[0:512, :] = (tr - top.astype(jnp.float32)).astype(jnp.bfloat16)
    pad = jnp.zeros((high.shape[0] - 512, 512), jnp.bfloat16)
    high[512:, :] = pad
    low_bits[512:, :] = pad
    project(node_v, 0, 512, 0, w1_v, ts)
    copies[2].wait()
    node_part[...] = dot(node_v[...], nw_top[...]) + nb1[...]
    copies[3].wait()


def early_kernel(bounds, recv_rows, edge, w1, b1, high, low_bits, part):
    def pair(p, carry):
        spreads = []
        for i in range(2):
            b = p * 2 + i
            span = pl.ds(pl.multiple_of(b * BLOCK, BLOCK), BLOCK)

            def spread(k, b=b):
                base = pl.multiple_of(bounds[b] + k * WINDOW, 8)
                hits = window_hits(base, recv_rows[b])
                rows = jnp.concatenate([high[pl.ds(base, WINDOW), :], low_bits[pl.ds(base, WINDOW), :]], axis=0)
                return lax.dot_general(
                    jnp.concatenate([hits, hits], axis=0), rows,
                    (((0,), (0,)), ((), ())), preferred_element_type=jnp.float32,
                )

            part[span, :] = 0.5 * (dot(edge[span, :], w1[0:512, :]) + b1[...]) + spread(0)
            spreads.append((b, span, spread))

        for b, span, spread in spreads:

            def more(k, c, span=span, spread=spread):
                part[span, :] += spread(k)
                return c

            lax.fori_loop(1, bounds[8 + b], more, 0)
        return carry

    lax.fori_loop(0, 4096 // BLOCK // 2, pair, 0)


def table_kernel(own, up, down, beside, w1, old_ts, ts):
    del old_ts
    project(own, 0, 1024, OWN, w1, ts)
    project(up, 0, 96, UP, w1, ts)
    project(down, 0, 96, DOWN, w1, ts)
    project(beside, 0, 96, NEXT, w1, ts)


def layer_kernel(
    send_ref, bounds,
    recv_rows, part, edge, node, swapped, old_ts, w1, w2, b2, gain, shift,
    node_part, nw1, nw2, nb2, ngain, nshift,
    edge_out, node_out, ts,
    g0, g1, hid0, hid1, y1, acc, outs, out_sems,
):
    blocks = 4096 // BLOCK
    live = bounds[16]
    del old_ts

    def span(b):
        return pl.ds(pl.multiple_of(b * BLOCK, BLOCK), BLOCK)

    def copy_out(b):
        return pltpu.make_async_copy(outs.at[span(b), :], edge_out.at[span(b), :], out_sems.at[b])

    def rows_at(lo):
        return pl.ds(pl.multiple_of(lo, CHUNK), CHUNK)

    project(swapped, 0, 1024, OTHER, w1, ts)
    project(swapped, 1024, 96, SWAP, w1, ts)
    acc[...] = jnp.zeros_like(acc)
    y1[...] = jnp.zeros_like(y1)

    def fetch16(i, carry):
        for e in range(16):
            for g, at in ((g0, 0), (g1, HALF)):
                s = pl.multiple_of(send_ref[at + i * 16 + e], 4)
                g[pl.ds(pl.multiple_of(i * 64 + e * 4, 4), 4), :] = ts[pl.ds(s, 4), :]
        return carry

    lax.fori_loop(0, HALF // 16, fetch16, 0)
    pieces = HALF // CHUNK

    def silu_piece(c, first, g, hid):
        lo = c * CHUNK
        for j in range(4):
            cols = slice(j * 128, j * 128 + 128)
            u = part[rows_at(first + lo), cols] + g[pl.ds(lo * 4 + j, CHUNK, stride=4), :]
            hid[lo : lo + CHUNK, cols] = half_silu(u)

    def norm_piece(c, first, y):
        lo = c * CHUNK
        update = normed(y[lo : lo + CHUNK, :] + b2[...], gain, shift)
        rows = rows_at(first + lo)
        outs[rows, :] = (edge[rows, :].astype(jnp.float32) + update).astype(jnp.bfloat16)

    def fetch_piece(c, source, g):
        for e in range(c * CHUNK, (c + 1) * CHUNK):
            s = pl.multiple_of(send_ref[source + e], 4)
            g[e * 4 : e * 4 + 4, :] = ts[pl.ds(s, 4), :]

    def finish(b):
        first = b * BLOCK

        @pl.when(first + BLOCK > live)
        def _():
            slot = first + lax.broadcasted_iota(jnp.int32, (BLOCK, 1), 0)
            outs[span(b), :] = jnp.where(slot < live, outs[span(b), :].astype(jnp.float32), 0.0).astype(jnp.bfloat16)

        copy_out(b).start()

        def add_window(k, carry):
            base = pl.multiple_of(bounds[b] + k * WINDOW, 8)
            acc[pl.ds(base, WINDOW), :] += dot(window_hits(base, recv_rows[b]), outs[span(b), :])
            return carry

        lax.fori_loop(0, bounds[8 + b], add_window, 0)

    def block(b, carry):
        first = b * BLOCK
        before = jnp.maximum(first - HALF, 0)
        for c in range(pieces):
            silu_piece(c, first, g0, hid0)
        y0 = dot(hid0[...], w2[...])
        for c in range(pieces):
            silu_piece(c, first + HALF, g1, hid1)
            fetch_piece(c, first + BLOCK, g0)
            norm_piece(c, before, y1)
        y_next = dot(hid1[...], w2[...])
        for c in range(pieces):
            norm_piece(c, first, y0)
            fetch_piece(c, first + BLOCK + HALF, g1)
        y1[...] = y_next

        @pl.when(b > 0)
        def _():
            finish(b - 1)

        return carry

    lax.fori_loop(0, blocks, block, 0)
    for c in range(pieces):
        norm_piece(c, 4096 - HALF, y1)
    finish(blocks - 1)
    pre = node_part[...] + dot(acc[0:512, :].astype(jnp.bfloat16), nw1[512:1024, :])
    update = normed(dot(half_silu(0.5 * pre), nw2[...]) + nb2[...], ngain, nshift)
    node_out[...] = (node[...].astype(jnp.float32) + update).astype(jnp.bfloat16)
    for b in range(blocks):
        copy_out(b).wait()


VMEM = pl.BlockSpec(memory_space=pltpu.VMEM)
SMEM = pl.BlockSpec(memory_space=pltpu.SMEM)
HBM = pl.BlockSpec(memory_space=pltpu.HBM)


def shape(rows, columns, dtype):
    return jax.ShapeDtypeStruct((rows, columns), dtype)


def params(mib):
    return pltpu.CompilerParams(vmem_limit_bytes=mib << 20)


def cost(rows, deep):
    return pl.CostEstimate(flops=rows * deep * 1024, bytes_accessed=rows * 3072, transcendentals=0)


def on_device(
    node_feat, edge_feat, sender, receiver, send_list,
    edge_w1, edge_b1, edge_w2, edge_b2, edge_gain, edge_shift,
    node_w1, node_b1, node_w2, node_b2, node_gain, node_shift,
):
    core = lax.axis_index("region") & 1
    barrier = lax.optimization_barrier
    row = lambda a: a.reshape(1, -1)
    ids = jnp.arange(512, dtype=jnp.int32)
    pick = (send_list.reshape(256, 1) == ids[None, :]).astype(jnp.bfloat16)
    rows = dot(pick, node_feat).astype(jnp.bfloat16)
    recv_rows = receiver.reshape(4096 // BLOCK, 1, BLOCK)
    b1 = row(edge_b1)

    table = shape(ROWS * 4, 128, jnp.float32)
    bf16, f32 = jnp.bfloat16, jnp.float32
    in_hbm = lambda a: pltpu.with_memory_space_constraint(a, pltpu.HBM)

    held = ring_phase(node_feat[:COARSE_DEV], 0)
    held, rows, recv_rows = barrier((held, rows, recv_rows))
    rows = rows.reshape(8, 32, 512)
    up = shifted([rows[4], rows[6], rows[2]], 8)
    down = shifted([rows[5], rows[3], rows[7]], -8)
    held = ring_phase(held, 1)
    node_v, w1_v, edge_v, high, low_bits, ts, node_part, bounds = pl.pallas_call(
        first_kernel,
        in_specs=[HBM] * 4 + [VMEM] * 2,
        out_specs=[VMEM] * 7 + [SMEM],
        out_shape=[
            shape(512, 512, bf16), shape(1536, 512, bf16), shape(4096, 512, bf16),
            shape(640, 512, bf16), shape(640, 512, bf16), table, shape(512, 512, f32),
            jax.ShapeDtypeStruct((32,), jnp.int32),
        ],
        scratch_shapes=[pltpu.VMEM((512, 512), bf16), pltpu.SemaphoreType.DMA((4,))],
        compiler_params=params(8),
        cost_estimate=cost(1536, 512),
    )(in_hbm(node_feat), in_hbm(edge_w1), in_hbm(node_w1), in_hbm(edge_feat), row(node_b1), recv_rows)
    held, up, down, node_v, high, sender = barrier((held, up, down, node_v, high, sender))

    to_right = jnp.concatenate([rows[0], up[32:64], down[32:64]], 0)
    to_left = jnp.concatenate([rows[1], up[64:96], down[64:96]], 0)
    across = [(i, (i + 1) % 128 if i & 1 else (i - 1) % 128) for i in range(128)]
    beside = lax.ppermute(jnp.where(core == 1, to_right, to_left), "region", across)
    own = ring_phase(held, 2)
    part = pl.pallas_call(
        early_kernel,
        in_specs=[SMEM] + [VMEM] * 6,
        out_specs=VMEM,
        out_shape=shape(4096, 512, f32),
        compiler_params=params(8),
        cost_estimate=cost(4096, 768),
    )(bounds, recv_rows, edge_v, w1_v, b1, high, low_bits)

    right = jnp.where(core == 0, NEXT, SWAP)
    left = jnp.where(core == 0, SWAP, NEXT)
    starts = (right, left, left + 32, right + 64, UP, DOWN, right + 32, left + 64)
    h = sender - 2560
    slot = h >> 5
    start = jnp.broadcast_to(starts[0], sender.shape).astype(jnp.int32)
    for j in range(1, 8):
        start = jnp.where(slot == j, starts[j], start)
    place = jnp.where(
        sender < 512,
        sender,
        jnp.where(sender < 2560, OWN + coarse_places(sender - 512), start + (h & 31)),
    )
    place = jnp.pad(place * 4, (0, BLOCK))
    own, beside, part, place = barrier((own, beside, part, place))

    inside = jnp.where(core == 0, to_right, to_left)
    swapped = lax.ppermute(
        jnp.concatenate([own, inside], 0), "region", [(i, i ^ 1) for i in range(128)]
    )
    ts = pl.pallas_call(
        table_kernel,
        in_specs=[VMEM] * 6,
        out_specs=VMEM,
        out_shape=table,
        input_output_aliases={5: 0},
        compiler_params=params(8),
        cost_estimate=cost(1312, 512),
    )(own, up, down, beside, w1_v, ts)

    edge_out, node_out, _ = pl.pallas_call(
        layer_kernel,
        in_specs=[SMEM] * 2 + [VMEM] * 17,
        out_specs=[HBM, VMEM, VMEM],
        out_shape=[shape(4096, 512, bf16), shape(512, 512, bf16), table],
        input_output_aliases={7: 2},
        scratch_shapes=[
            pltpu.VMEM((HALF * 4, 128), f32),
            pltpu.VMEM((HALF * 4, 128), f32),
            pltpu.VMEM((HALF, 512), bf16),
            pltpu.VMEM((HALF, 512), bf16),
            pltpu.VMEM((HALF, 512), f32),
            pltpu.VMEM((640, 512), f32),
            pltpu.VMEM((4096, 512), bf16),
            pltpu.SemaphoreType.DMA((4096 // BLOCK,)),
        ],
        compiler_params=params(20),
    )(
        place, bounds, recv_rows, part, edge_v, node_v, swapped, ts, w1_v,
        edge_w2, row(edge_b2), row(edge_gain), row(edge_shift),
        node_part, node_w1, node_w2, row(node_b2), row(node_gain), row(node_shift),
    )
    return edge_out, node_out


def solution(mesh):
    sharded = {0: P("region", None), 1: P("region", None), 2: P("region"), 3: P("region"), 4: P("region", None, None)}
    in_specs = tuple(sharded.get(i, P()) for i in range(17))
    out_specs = (P("region", None), P("region", None))
    step = lambda *a: tuple(on_device(*a))
    return jax.shard_map(step, mesh=mesh, in_specs=in_specs, out_specs=out_specs, check_vma=False)
```

```python
import jax
import jax.numpy as jnp
from jax import lax
from jax.experimental import pallas as pl
from jax.experimental.pallas import tpu as pltpu
from jax.sharding import PartitionSpec as P

COARSE_DEV = 16
BLOCK = 512
WINDOW = 128
HALF = BLOCK // 2
CHUNK = 64
OWN, OTHER, UP, DOWN, NEXT, SWAP, ROWS = 512, 1536, 2560, 2656, 2752, 2848, 2944
PHASES = ((2, 1, 0), (0, 2, 1))


def coords_of(region):
    return [region >> 5 & 3, region >> 3 & 3, region >> 1 & 3, region & 1]


def region_of(x, y, z, core):
    return ((x * 4 + y) * 4 + z) * 2 + core


def ring_route(phase, step):
    route = []
    for region in range(128):
        place = coords_of(region)
        dim = PHASES[place[3]][phase]
        place[dim] = (place[dim] + step) % 4
        route.append((region, region_of(*place)))
    return route


def linear_route(step):
    return [(i, (i + step) % 128) for i in range(128)]


def ring_phase(held, phase):
    parts = [held]
    parts += [lax.ppermute(held, "region", ring_route(phase, k)) for k in (1, 2, 3)]
    return jnp.concatenate(parts, axis=0)


def shifted(blocks, step):
    return lax.ppermute(jnp.concatenate(blocks, 0), "region", linear_route(step))


def coarse_places(index):
    me = lax.axis_index("region")
    mine = coords_of(me)
    row = index & 15
    theirs = coords_of(index >> 4)
    rel = [(mine[d] - theirs[d]) & 3 for d in range(3)]
    order = [(rel[c] * 16 + rel[b] * 4 + rel[a]) for a, b, c in PHASES]
    block = jnp.where(theirs[3] == 0, order[0], order[1])
    return jnp.where(theirs[3] == mine[3], 0, 1024) + block * 16 + row


def normed(y, gain_ref, shift_ref):
    mean = jnp.mean(y, axis=-1, keepdims=True)
    d = y - mean
    var = jnp.mean(d * d, axis=-1, keepdims=True)
    return d * lax.rsqrt(var + 1e-05) * gain_ref[...] + shift_ref[...]


def half_silu(u):
    return (u + u * jnp.tanh(u)).astype(jnp.bfloat16)


def dot(a, b):
    return jnp.dot(a, b, preferred_element_type=jnp.float32)


def window_hits(base, recv_row):
    ids = base + lax.broadcasted_iota(jnp.int32, (WINDOW, BLOCK), 0)
    return jnp.where(ids == recv_row, 1.0, 0.0).astype(jnp.bfloat16)


def project(src, lo, count, at, w1, ts):
    for r in range(0, count, 256):
        n = min(256, count - r)
        res = 0.5 * dot(src[lo + r : lo + r + n, :], w1[512:1024, :])
        for j in range(4):
            ts[pl.ds((at + r) * 4 + j, n, stride=4), :] = res[:, j * 128 : j * 128 + 128]


def first_kernel(
    node, w1, nw1, recv_rows, picks,
    node_v, w1_v, recv_v, high, low_bits, ts, node_part, rows, bounds,
    nw_top, sems,
):
    moves = [(recv_rows, recv_v), (node, node_v), (w1, w1_v), (nw1.at[0:512, :], nw_top)]
    copies = [pltpu.make_async_copy(a, b, sems.at[i]) for i, (a, b) in enumerate(moves)]
    for copy in copies:
        copy.start()
    ids = lax.broadcasted_iota(jnp.int32, (512, 256), 0)
    chosen = jnp.where(ids == picks[...], 1.0, 0.0).astype(jnp.bfloat16)
    copies[0].wait()
    recv = recv_v[:, 0, :]
    bounds[16] = jnp.sum(jnp.where(recv < 512, 1, 0))
    for b in range(4096 // BLOCK):
        low = jnp.min(recv[b : b + 1, :]) >> 3 << 3
        bounds[b] = low
        bounds[8 + b] = (jnp.max(recv[b : b + 1, :]) - low) // WINDOW + 1
    copies[1].wait()
    rows[...] = lax.dot_general(
        chosen, node_v[...], (((0,), (0,)), ((), ())), preferred_element_type=jnp.float32
    ).astype(jnp.bfloat16)
    copies[2].wait()
    tr = 0.5 * dot(node_v[...], w1_v[1024:1536, :])
    top = tr.astype(jnp.bfloat16)
    high[0:512, :] = top
    low_bits[0:512, :] = (tr - top.astype(jnp.float32)).astype(jnp.bfloat16)
    pad = jnp.zeros((high.shape[0] - 512, 512), jnp.bfloat16)
    high[512:, :] = pad
    low_bits[512:, :] = pad
    project(node_v, 0, 512, 0, w1_v, ts)
    copies[3].wait()
    node_part[...] = dot(node_v[...], nw_top[...])


def early_kernel(bounds, recv_rows, edge, w1, b1, high, low_bits, part, edge_v, sems):
    def span_of(b):
        return pl.ds(pl.multiple_of(b * BLOCK, BLOCK), BLOCK)

    def copy(b):
        return pltpu.make_async_copy(edge.at[span_of(b), :], edge_v.at[span_of(b), :], sems.at[b])

    for b in range(4096 // BLOCK):
        copy(b).start()

    def pair(p, carry):
        copy(p * 2).wait()
        copy(p * 2 + 1).wait()
        spreads = []
        for i in range(2):
            b = p * 2 + i
            span = span_of(b)

            def spread(k, b=b):
                base = pl.multiple_of(bounds[b] + k * WINDOW, 8)
                hits = window_hits(base, recv_rows[b])
                rows = jnp.concatenate([high[pl.ds(base, WINDOW), :], low_bits[pl.ds(base, WINDOW), :]], axis=0)
                return lax.dot_general(
                    jnp.concatenate([hits, hits], axis=0), rows,
                    (((0,), (0,)), ((), ())), preferred_element_type=jnp.float32,
                )

            part[span, :] = 0.5 * (dot(edge_v[span, :], w1[0:512, :]) + b1[...]) + spread(0)
            spreads.append((b, span, spread))

        for b, span, spread in spreads:

            def more(k, c, span=span, spread=spread):
                part[span, :] += spread(k)
                return c

            lax.fori_loop(1, bounds[8 + b], more, 0)
        return carry

    lax.fori_loop(0, 4096 // BLOCK // 2, pair, 0)


def table_kernel(own, up, down, w1, old_ts, ts):
    del old_ts
    project(own, 0, 1024, OWN, w1, ts)
    project(up, 0, 96, UP, w1, ts)
    project(down, 0, 96, DOWN, w1, ts)


def layer_kernel(
    send_ref, bounds,
    recv_rows, part, edge, node, swapped, beside, old_ts, w1, w2, b2, gain, shift,
    node_part, nw1, nb1, nw2, nb2, ngain, nshift,
    edge_out, node_out, ts,
    g0, g1, hid0, hid1, y1, acc, outs, out_sems,
):
    blocks = 4096 // BLOCK
    live = bounds[16]
    del old_ts

    def span(b):
        return pl.ds(pl.multiple_of(b * BLOCK, BLOCK), BLOCK)

    def copy_out(b):
        return pltpu.make_async_copy(outs.at[span(b), :], edge_out.at[span(b), :], out_sems.at[b])

    def rows_at(lo):
        return pl.ds(pl.multiple_of(lo, CHUNK), CHUNK)

    project(swapped, 0, 1024, OTHER, w1, ts)
    project(swapped, 1024, 96, SWAP, w1, ts)
    project(beside, 0, 96, NEXT, w1, ts)
    acc[...] = jnp.zeros_like(acc)
    y1[...] = jnp.zeros_like(y1)

    def fetch16(i, carry):
        for e in range(16):
            s = pl.multiple_of(send_ref[i * 16 + e], 4)
            g0[pl.ds(pl.multiple_of(i * 64 + e * 4, 4), 4), :] = ts[pl.ds(s, 4), :]
        return carry

    lax.fori_loop(0, HALF // 16, fetch16, 0)
    pieces = HALF // CHUNK

    def silu_piece(c, first, g, hid):
        lo = c * CHUNK
        for j in range(4):
            cols = slice(j * 128, j * 128 + 128)
            u = part[rows_at(first + lo), cols] + g[pl.ds(lo * 4 + j, CHUNK, stride=4), :]
            hid[lo : lo + CHUNK, cols] = half_silu(u)

    def norm_piece(c, first, y):
        lo = c * CHUNK
        update = normed(y[lo : lo + CHUNK, :] + b2[...], gain, shift)
        rows = rows_at(first + lo)
        outs[rows, :] = (edge[rows, :].astype(jnp.float32) + update).astype(jnp.bfloat16)

    def fetch_piece(c, source, g):
        for e in range(c * CHUNK, (c + 1) * CHUNK):
            s = pl.multiple_of(send_ref[source + e], 4)
            g[e * 4 : e * 4 + 4, :] = ts[pl.ds(s, 4), :]

    def finish(b):
        first = b * BLOCK

        @pl.when(first + BLOCK > live)
        def _():
            slot = first + lax.broadcasted_iota(jnp.int32, (BLOCK, 1), 0)
            outs[span(b), :] = jnp.where(slot < live, outs[span(b), :].astype(jnp.float32), 0.0).astype(jnp.bfloat16)

        copy_out(b).start()

        def add_window(k, carry):
            base = pl.multiple_of(bounds[b] + k * WINDOW, 8)
            acc[pl.ds(base, WINDOW), :] += dot(window_hits(base, recv_rows[b]), outs[span(b), :])
            return carry

        lax.fori_loop(0, bounds[8 + b], add_window, 0)

    def block(b, carry):
        first = b * BLOCK
        before = jnp.maximum(first - HALF, 0)
        for c in range(pieces):
            silu_piece(c, first, g0, hid0)
            fetch_piece(c, first + HALF, g1)
        y0 = dot(hid0[...], w2[...])
        for c in range(pieces):
            silu_piece(c, first + HALF, g1, hid1)
            fetch_piece(c, first + BLOCK, g0)
            norm_piece(c, before, y1)
        y_next = dot(hid1[...], w2[...])
        for c in range(pieces):
            norm_piece(c, first, y0)
        y1[...] = y_next

        @pl.when(b > 0)
        def _():
            finish(b - 1)

        return carry

    busy = (live + BLOCK - 1) // BLOCK
    lax.fori_loop(0, busy, block, 0)

    @pl.when(busy > 0)
    def _():
        for c in range(pieces):
            norm_piece(c, busy * BLOCK - HALF, y1)
        finish(busy - 1)

    def empty(b, carry):
        outs[span(b), :] = jnp.zeros((BLOCK, 512), jnp.bfloat16)
        copy_out(b).start()
        return carry

    lax.fori_loop(busy, blocks, empty, 0)
    pre = node_part[...] + dot(acc[0:512, :].astype(jnp.bfloat16), nw1[512:1024, :]) + nb1[...]
    update = normed(dot(half_silu(0.5 * pre), nw2[...]) + nb2[...], ngain, nshift)
    node_out[...] = (node[...].astype(jnp.float32) + update).astype(jnp.bfloat16)
    for b in range(blocks):
        copy_out(b).wait()


VMEM = pl.BlockSpec(memory_space=pltpu.VMEM)
SMEM = pl.BlockSpec(memory_space=pltpu.SMEM)
HBM = pl.BlockSpec(memory_space=pltpu.HBM)


def shape(rows, columns, dtype):
    return jax.ShapeDtypeStruct((rows, columns), dtype)


def params(mib):
    return pltpu.CompilerParams(vmem_limit_bytes=mib << 20)


def cost(rows, deep):
    return pl.CostEstimate(flops=rows * deep * 1024, bytes_accessed=rows * 3072, transcendentals=0)


def on_device(
    node_feat, edge_feat, sender, receiver, send_list,
    edge_w1, edge_b1, edge_w2, edge_b2, edge_gain, edge_shift,
    node_w1, node_b1, node_w2, node_b2, node_gain, node_shift,
):
    core = lax.axis_index("region") & 1
    barrier = lax.optimization_barrier
    row = lambda a: a.reshape(1, -1)
    picks = send_list.reshape(1, 256)
    recv_rows = receiver.reshape(4096 // BLOCK, 1, BLOCK)
    b1 = row(edge_b1)

    table = shape(ROWS * 4, 128, jnp.float32)
    bf16, f32 = jnp.bfloat16, jnp.float32
    in_hbm = lambda a: pltpu.with_memory_space_constraint(a, pltpu.HBM)

    held = ring_phase(node_feat[:COARSE_DEV], 0)
    held, picks = barrier((held, picks))
    held = ring_phase(held, 1)
    node_v, w1_v, recv_v, high, low_bits, ts, node_part, rows, bounds = pl.pallas_call(
        first_kernel,
        in_specs=[HBM] * 4 + [VMEM],
        out_specs=[VMEM] * 8 + [SMEM],
        out_shape=[
            shape(512, 512, bf16), shape(1536, 512, bf16), jax.ShapeDtypeStruct(recv_rows.shape, jnp.int32),
            shape(640, 512, bf16), shape(640, 512, bf16), table, shape(512, 512, f32), shape(256, 512, bf16),
            jax.ShapeDtypeStruct((32,), jnp.int32),
        ],
        scratch_shapes=[pltpu.VMEM((512, 512), bf16), pltpu.SemaphoreType.DMA((4,))],
        compiler_params=params(8),
        cost_estimate=cost(1792, 512),
    )(in_hbm(node_feat), in_hbm(edge_w1), in_hbm(node_w1), in_hbm(recv_rows), picks)
    held, rows, node_v, high, sender = barrier((held, rows, node_v, high, sender))

    rows = rows.reshape(8, 32, 512)
    up = shifted([rows[4], rows[6], rows[2]], 8)
    down = shifted([rows[5], rows[3], rows[7]], -8)
    own = ring_phase(held, 2)
    part, edge_v = pl.pallas_call(
        early_kernel,
        in_specs=[SMEM, VMEM, HBM] + [VMEM] * 4,
        out_specs=[VMEM, VMEM],
        out_shape=[shape(4096, 512, f32), shape(4096, 512, bf16)],
        scratch_shapes=[pltpu.SemaphoreType.DMA((4096 // BLOCK,))],
        compiler_params=params(8),
        cost_estimate=cost(4096, 768),
    )(bounds, recv_v, in_hbm(edge_feat), w1_v, b1, high, low_bits)

    right = jnp.where(core == 0, NEXT, SWAP)
    left = jnp.where(core == 0, SWAP, NEXT)
    starts = (right, left, left + 32, right + 64, UP, DOWN, right + 32, left + 64)
    h = sender - 2560
    slot = h >> 5
    start = jnp.broadcast_to(starts[0], sender.shape).astype(jnp.int32)
    for j in range(1, 8):
        start = jnp.where(slot == j, starts[j], start)
    place = jnp.where(
        sender < 512,
        sender,
        jnp.where(sender < 2560, OWN + coarse_places(sender - 512), start + (h & 31)),
    )
    place = jnp.pad(place * 4, (0, BLOCK))
    own, up, down, part, place = barrier((own, up, down, part, place))

    to_right = jnp.concatenate([rows[0], up[32:64], down[32:64]], 0)
    to_left = jnp.concatenate([rows[1], up[64:96], down[64:96]], 0)
    inside = jnp.where(core == 0, to_right, to_left)
    swapped = lax.ppermute(
        jnp.concatenate([own, inside], 0), "region", [(i, i ^ 1) for i in range(128)]
    )
    across = [(i, (i + 1) % 128 if i & 1 else (i - 1) % 128) for i in range(128)]
    beside = lax.ppermute(jnp.where(core == 1, to_right, to_left), "region", across)
    ts = pl.pallas_call(
        table_kernel,
        in_specs=[VMEM] * 5,
        out_specs=VMEM,
        out_shape=table,
        input_output_aliases={4: 0},
        compiler_params=params(8),
        cost_estimate=cost(1216, 512),
    )(own, up, down, w1_v, ts)

    edge_out, node_out, _ = pl.pallas_call(
        layer_kernel,
        in_specs=[SMEM] * 2 + [VMEM] * 19,
        out_specs=[HBM, VMEM, VMEM],
        out_shape=[shape(4096, 512, bf16), shape(512, 512, bf16), table],
        input_output_aliases={8: 2},
        scratch_shapes=[
            pltpu.VMEM((HALF * 4, 128), f32),
            pltpu.VMEM((HALF * 4, 128), f32),
            pltpu.VMEM((HALF, 512), bf16),
            pltpu.VMEM((HALF, 512), bf16),
            pltpu.VMEM((HALF, 512), f32),
            pltpu.VMEM((640, 512), f32),
            pltpu.VMEM((4096, 512), bf16),
            pltpu.SemaphoreType.DMA((4096 // BLOCK,)),
        ],
        compiler_params=params(20),
    )(
        place, bounds, recv_v, part, edge_v, node_v, swapped, beside, ts, w1_v,
        edge_w2, row(edge_b2), row(edge_gain), row(edge_shift),
        node_part, node_w1, row(node_b1), node_w2, row(node_b2), row(node_gain), row(node_shift),
    )
    return edge_out, node_out


def solution(mesh):
    sharded = {0: P("region", None), 1: P("region", None), 2: P("region"), 3: P("region"), 4: P("region", None, None)}
    in_specs = tuple(sharded.get(i, P()) for i in range(17))
    out_specs = (P("region", None), P("region", None))
    step = lambda *a: tuple(on_device(*a))
    return jax.shard_map(step, mesh=mesh, in_specs=in_specs, out_specs=out_specs, check_vma=False)
```
